256 devices in a mesh: row: 32 (over x, z), col: 8 (over y, core).
Axes of the slice: x: 4, y: 4, z: 8, core: 2. Of those that a mesh axis runs over, the one named last changes fastest.
Arguments:
- tensor: bfloat16 [64, 2048, 2048], P(None, 'row', 'col'), may hold values from -6 to 6
- pattern: int32 [32, 32], P('col', 'row'), may hold values 0 or 1
- coef: bfloat16 [2048, 2048], P('row', 'col'), may hold values from -0.1875 to 0.1875
Outputs:
- contracted: bfloat16 [64, 2048, 2048], P(None, 'row', 'col')
The draws below stay inside these ranges and needn't reach their ends.
All inputs are finite; a program needn't handle non-finite values. No bound on the sum of `pattern` on one device may be relied on, other than what follows from the above.
Results may differ from the reference program's by a relative error of at most 0.001.
Values may be sent and summed in bfloat16 or wider, within the bound.
A program may use at most 64 MiB of HBM per device.

```python
import jax
import jax.numpy as jnp
from jax import lax

BLK = 64
AUX = 2048
ORB = 2048
MU = 64
NU = 2048


def set_ends(values, stream_key, least, high):
    longest = values.shape.index(max(values.shape))
    spots = []
    for shift in (0, 1):
        where = [jax.random.randint(jax.random.fold_in(stream_key, axis), (), 0, length) for axis, length in enumerate(values.shape)]
        where[longest] = (where[longest] + shift) % values.shape[longest]
        spots.append(tuple(where))
    return values.at[spots[0]].set(least).at[spots[1]].set(high)


def shard_levels(rng, shape, shards, least, largest):
    loudness = 1.0
    for axis_at, shards_of in shards:
        draws = jax.random.uniform(jax.random.fold_in(jax.random.fold_in(rng, 6), axis_at), (shards_of,), jnp.float32, least / len(shards), largest / len(shards))
        loudness = loudness * jnp.repeat(jnp.exp(draws), shape[axis_at] // shards_of).reshape((-1,) + (1,) * (len(shape) - 1 - axis_at))
    return loudness


def gaussian(own_key, shape, scale, reach, cuts=(), kind=jnp.bfloat16):
    drawn = scale * jax.random.normal(own_key, shape, jnp.float32)
    if cuts:
        drawn = drawn * shard_levels(own_key, shape, cuts, -0.22, 0.18)
    return jnp.clip(drawn, -reach, reach).astype(kind)


def setup_inputs(seed: int = 0) -> dict:
    streams_of = jax.random.split(jax.random.key(seed), 4)
    return {
        "tensor": gaussian(streams_of[0], (MU, NU, AUX), 1.0, 6.0, ((1, 32), (2, 8))),
        "pattern": set_ends((jax.random.randint(streams_of[1], (AUX // BLK, NU // BLK), 0, 2) < 1).astype(jnp.int32), jax.random.fold_in(streams_of[1], 1), 0, 1),
        "coef": gaussian(streams_of[2], (NU, ORB), (NU // 2) ** -0.5, 0.1875, ((0, 32), (1, 8))),
    }


def reference(tensor, pattern, coef):
    mu, nu, aux = tensor.shape
    atoms = pattern.shape[0]
    blk = aux // atoms
    coef_wide = coef.astype(jnp.float32)

    def one_block(index):
        rows = lax.dynamic_slice_in_dim(tensor, index * blk, blk, 2)
        keep = lax.dynamic_slice_in_dim(pattern, index, 1, 0)[0]
        wide = jnp.repeat(keep, blk).astype(jnp.bfloat16)
        masked = rows * wide[None, :, None]
        prod = jnp.einsum("mna,no->moa", masked.astype(jnp.float32), coef_wide)
        return prod.astype(jnp.bfloat16)

    result = lax.map(one_block, jnp.arange(atoms, dtype=jnp.int32))
    result = jnp.transpose(result, (1, 2, 0, 3))
    return result.reshape(mu, coef.shape[1], aux)
```

```python
import jax
import jax.numpy as jnp
from jax import lax
from jax.experimental import pallas as pl
from jax.experimental.pallas import tpu as pltpu
from jax.sharding import PartitionSpec as P

MESH = pl.DeviceIdType.MESH
X, Y, Z, CORES = 4, 4, 8, 2
ROWS, COLS = X * Z, Y * CORES


def kernel(
    pattern, tensor, coef, out,
    raw, masked, matrix, whole, result,
    load_sem, own_sem, send_sem, matrix_sem, out_sem,
    coef_send, z_sem, x_sem, y_sem, relay_sem, core_sem,
):
    atoms, blk = pattern.shape[0], tensor.shape[2] // pattern.shape[0]
    mu_all, nu_loc, aux_loc = tensor.shape
    mu_per = mu_all // ROWS
    row, col = lax.axis_index("row"), lax.axis_index("col")
    x, z = row // Z, lax.rem(row, Z)
    y, core = col // CORES, lax.rem(col, CORES)

    def at(dx, dz):
        return lax.rem(x + dx, X) * Z + lax.rem(z + dz, Z)

    def col_at(dy):
        return lax.rem(y + dy, Y) * CORES + core

    partner = y * CORES + (1 - core)

    loads = []
    step = mu_all // 4
    for q in range(4):
        part = pl.ds(q * step, step)
        load = pltpu.make_async_copy(tensor.at[part], raw.at[part], load_sem.at[q])
        load.start()
        loads.append(load)
    n_rows = pl.ds(pl.multiple_of(row * nu_loc, nu_loc), nu_loc)
    own_coef = pltpu.make_async_copy(coef, whole.at[col, n_rows], load_sem.at[4])
    own_coef.start()

    barrier = pltpu.get_barrier_semaphore()

    def greet(k, carry):
        pl.semaphore_signal(
            barrier, 1, device_id={"row": at(k // Z, lax.rem(k, Z))}, device_id_type=MESH
        )
        return carry

    lax.fori_loop(1, ROWS, greet, 0)
    for dy in range(1, Y):
        pl.semaphore_signal(barrier, 1, device_id={"col": col_at(dy)}, device_id_type=MESH)
    pl.semaphore_signal(barrier, 1, device_id={"col": partner}, device_id_type=MESH)

    lane = lax.broadcasted_iota(jnp.int32, (1, 1, aux_loc), 2)
    keep = jnp.zeros((1, 1, aux_loc), jnp.float32)
    for a in range(atoms):
        here = (lane >= a * blk) & (lane < (a + 1) * blk)
        keep = jnp.where(here, pattern[a, 0].astype(jnp.float32), keep)
    keep = keep.astype(jnp.bfloat16)
    for q in range(4):
        loads[q].wait()

        def mask(i, carry):
            some = pl.ds(q * step + i * 2, 2)
            masked[some] = raw[some] * keep
            return carry

        lax.fori_loop(0, step // 2, mask, 0)
    own_coef.wait()
    pl.semaphore_wait(barrier, ROWS - 1 + Y - 1 + 1)

    def send_coef(stage, rows, which, sem, **device):
        block = whole.at[which, rows]
        copy = pltpu.make_async_remote_copy(
            block, block, coef_send.at[stage], sem, device_id=device, device_id_type=MESH
        )
        copy.start()

    for dz in range(1, Z):
        send_coef(0, n_rows, col, z_sem, row=at(0, dz))

    for m in range(mu_per):

        def send_block(k, carry):
            peer = at(k // Z, lax.rem(k, Z))
            pltpu.make_async_remote_copy(
                masked.at[peer * mu_per + m], matrix.at[m, n_rows], send_sem.at[0],
                matrix_sem.at[m], device_id={"row": peer}, device_id_type=MESH,
            ).start()
            return carry

        lax.fori_loop(1, ROWS, send_block, 0)
        pltpu.make_async_copy(
            masked.at[row * mu_per + m], matrix.at[m, n_rows], own_sem.at[m]
        ).start()

    slab = Z * nu_loc

    def x_rows(dx):
        return pl.ds(pl.multiple_of(lax.rem(x + dx, X) * slab, slab), slab)

    def wait_rows(count, sem):
        block = whole.at[0, pl.ds(0, count)]
        pltpu.make_async_copy(block, block, sem).wait()

    def spread(dx):
        rows = x_rows(dx)
        send_coef(2, rows, col, y_sem.at[0, dx], col=col_at(1))
        send_coef(2, rows, col, y_sem.at[1, dx], col=col_at(Y - 1))
        send_coef(4, rows, col, core_sem, col=partner)

    wait_rows((Z - 1) * nu_loc, z_sem)
    for dx in (1, 3, 2):
        send_coef(1, x_rows(0), col, x_sem.at[dx - 1], row=at(dx, 0))
    spread(0)
    for s in (1, 3, 2):
        wait_rows(slab, x_sem.at[s - 1])
        spread(X - s)
    for i, dx in enumerate((0, 3, 1, 2)):
        rows = x_rows(dx)
        wait_rows(slab, y_sem.at[0, dx])
        if i < 2:
            send_coef(3, rows, col_at(Y - 1), relay_sem.at[0, i], col=col_at(1))
        send_coef(4, rows, col_at(Y - 1), core_sem, col=partner)
        wait_rows(slab, y_sem.at[1, dx])
        if i >= 2:
            send_coef(3, rows, col_at(1), relay_sem.at[1, i - 2], col=col_at(Y - 1))
        send_coef(4, rows, col_at(1), core_sem, col=partner)
    for i, dx in enumerate((0, 3, 1, 2)):
        wait_rows(slab, relay_sem.at[i // 2, i % 2])
        send_coef(4, x_rows(dx), col_at(2), core_sem, col=partner)
    half = whole.at[pl.ds(0, Y)]
    pltpu.make_async_copy(half, half, core_sem).wait()

    for m in range(mu_per):
        own = pltpu.make_async_copy(
            masked.at[row * mu_per + m], matrix.at[m, n_rows], own_sem.at[m]
        )
        own.wait()
        most = matrix.at[m, pl.ds(0, (ROWS - 1) * nu_loc)]
        pltpu.make_async_copy(most, most, matrix_sem.at[m]).wait()
        per = aux_loc // nu_loc

        def tile(k, carry):
            t = lax.rem(row // per + k, COLS)
            product = lax.dot_general(
                whole[t], matrix[m], (((0,), (0,)), ((), ())),
                preferred_element_type=jnp.float32,
            )
            result[m, pl.ds(pl.multiple_of(t * aux_loc, aux_loc), aux_loc)] = product.astype(
                jnp.bfloat16
            )
            for j in range(per):
                peer = t * per + j

                @pl.when(peer != row)
                def _():
                    pltpu.make_async_remote_copy(
                        result.at[m, pl.ds(pl.multiple_of(peer * nu_loc, nu_loc), nu_loc)],
                        out.at[row * mu_per + m], send_sem.at[1], out_sem,
                        device_id={"row": peer}, device_id_type=MESH,
                    ).start()

            return carry

        lax.fori_loop(0, COLS, tile, 0)
        pltpu.make_async_copy(
            result.at[m, n_rows], out.at[row * mu_per + m], own_sem.at[m]
        ).start()

    for m in range(mu_per):
        pltpu.make_async_copy(
            result.at[m, n_rows], out.at[row * mu_per + m], own_sem.at[m]
        ).wait()
    most = masked.at[pl.ds(0, (ROWS - 1) * mu_per)]
    pltpu.make_async_copy(most, most, out_sem).wait()
    pltpu.make_async_copy(most, most, send_sem.at[0]).wait()
    pltpu.make_async_copy(most, most, send_sem.at[1]).wait()
    wait_rows((Z - 1) * nu_loc, coef_send.at[0])
    wait_rows((X - 1) * slab, coef_send.at[1])
    quarter = whole.at[pl.ds(0, 2)]
    pltpu.make_async_copy(quarter, quarter, coef_send.at[2]).wait()
    wait_rows(X * slab, coef_send.at[3])
    pltpu.make_async_copy(half, half, coef_send.at[4]).wait()


def per_device(tensor, pattern, coef):
    mu_all, nu_loc, aux_loc = tensor.shape
    mu_per = mu_all // ROWS
    nu_all = nu_loc * ROWS
    dma = pltpu.SemaphoreType.DMA
    return pl.pallas_call(
        kernel,
        out_shape=jax.ShapeDtypeStruct(tensor.shape, jnp.bfloat16),
        in_specs=[
            pl.BlockSpec(memory_space=pltpu.SMEM),
            pl.BlockSpec(memory_space=pl.ANY),
            pl.BlockSpec(memory_space=pl.ANY),
        ],
        out_specs=pl.BlockSpec(memory_space=pl.ANY),
        scratch_shapes=[
            pltpu.VMEM(tensor.shape, jnp.bfloat16),
            pltpu.VMEM(tensor.shape, jnp.bfloat16),
            pltpu.VMEM((mu_per, nu_all, aux_loc), jnp.bfloat16),
            pltpu.VMEM((COLS, nu_all, aux_loc), jnp.bfloat16),
            pltpu.VMEM((mu_per, nu_all, aux_loc), jnp.bfloat16),
            dma((5,)), dma((mu_per,)), dma((2,)), dma((mu_per,)), dma(()),
            dma((5,)), dma(()), dma((X - 1,)), dma((2, X)), dma((2, 2)), dma(()),
        ],
        compiler_params=pltpu.CompilerParams(
            collective_id=0, has_side_effects=True, vmem_limit_bytes=40 * 1024 * 1024
        ),
    )(pattern, tensor, coef)


def solution(mesh):
    return jax.shard_map(
        per_device,
        mesh=mesh,
        in_specs=(P(None, "row", "col"), P("col", "row"), P("row", "col")),
        out_specs=P(None, "row", "col"),
        check_vma=False,
    )
```

```python
import jax
import jax.numpy as jnp
from jax import lax
from jax.experimental import pallas as pl
from jax.experimental.pallas import tpu as pltpu
from jax.sharding import PartitionSpec as P

MESH = pl.DeviceIdType.MESH
X, Y, Z, CORES = 4, 4, 8, 2
ROWS, COLS = X * Z, Y * CORES
SPLIT = 6


def kernel(
    pattern_hbm, tensor, coef, out,
    pattern, raw, masked, matrix, whole, result,
    load_sem, own_sem, send_sem, matrix_sem, out_sem,
    coef_send, z_sem, x_sem, y_sem, relay_sem, core_sem,
):
    atoms = pattern.shape[1]
    blk = tensor.shape[2] // atoms
    mu_all, nu_loc, aux_loc = tensor.shape
    mu_per = mu_all // ROWS
    row, col = lax.axis_index("row"), lax.axis_index("col")
    x, z = row // Z, lax.rem(row, Z)
    y, core = col // CORES, lax.rem(col, CORES)

    def at(dx, dz):
        return lax.rem(x + dx, X) * Z + lax.rem(z + dz, Z)

    def col_at(dy):
        return lax.rem(y + dy, Y) * CORES + core

    partner = y * CORES + (1 - core)

    own_pattern = pltpu.make_async_copy(pattern_hbm, pattern, load_sem.at[5])
    own_pattern.start()
    n_rows = pl.ds(pl.multiple_of(row * nu_loc, nu_loc), nu_loc)
    own_coef = pltpu.make_async_copy(coef, whole.at[col, n_rows], load_sem.at[4])
    own_coef.start()
    loads = []
    step = mu_all // 4
    for q in range(4):
        part = pl.ds(q * step, step)
        load = pltpu.make_async_copy(tensor.at[part], raw.at[part], load_sem.at[q])
        load.start()
        loads.append(load)

    barrier = pltpu.get_barrier_semaphore()
    hops = lambda d, n: min(d, n - d)
    peers = [(dx, dz) for dx in range(X) for dz in range(Z) if dx or dz]
    for dx, dz in sorted(peers, key=lambda o: -hops(o[0], X) - hops(o[1], Z)):
        pl.semaphore_signal(barrier, 1, device_id={"row": at(dx, dz)}, device_id_type=MESH)
    for dy in range(1, Y):
        pl.semaphore_signal(barrier, 1, device_id={"col": col_at(dy)}, device_id_type=MESH)
    pl.semaphore_signal(barrier, 1, device_id={"col": partner}, device_id_type=MESH)

    own_pattern.wait()
    lane = lax.broadcasted_iota(jnp.int32, (1, 1, aux_loc), 2)
    keep = jnp.zeros((1, 1, aux_loc), jnp.float32)
    for a in range(atoms):
        here = (lane >= a * blk) & (lane < (a + 1) * blk)
        keep = jnp.where(here, pattern[0, a].astype(jnp.float32), keep)
    keep = keep.astype(jnp.bfloat16)
    own_coef.wait()
    for q in range(4):
        loads[q].wait()

        def mask(i, carry):
            some = pl.ds(q * step + i * 2, 2)
            masked[some] = raw[some] * keep
            return carry

        lax.fori_loop(0, step // 2, mask, 0)
    pl.semaphore_wait(barrier, ROWS - 1 + Y - 1 + 1)

    def send_coef(stage, rows, which, sem, **device):
        block = whole.at[which, rows]
        copy = pltpu.make_async_remote_copy(
            block, block, coef_send.at[stage], sem, device_id=device, device_id_type=MESH
        )
        copy.start()

    for dz in range(1, Z):
        send_coef(0, n_rows, col, z_sem, row=at(0, dz))

    for m in range(mu_per):

        def send_block(k, carry):
            peer = at(k // Z, lax.rem(k, Z))
            pltpu.make_async_remote_copy(
                masked.at[peer * mu_per + m], matrix.at[m, n_rows], send_sem.at[0],
                matrix_sem.at[m], device_id={"row": peer}, device_id_type=MESH,
            ).start()
            return carry

        lax.fori_loop(1, ROWS, send_block, 0)
        pltpu.make_async_copy(
            masked.at[row * mu_per + m], matrix.at[m, n_rows], own_sem.at[m]
        ).start()

    slab, first = Z * nu_loc, SPLIT * nu_loc
    sizes = (first, slab - first)

    def rows_of(g, dx):
        start = lax.rem(x + dx, X) * slab + g * first
        return pl.ds(pl.multiple_of(start, nu_loc), sizes[g])

    def wait_rows(count, sem):
        block = whole.at[0, pl.ds(0, count)]
        pltpu.make_async_copy(block, block, sem).wait()

    def one(g, d):
        return (rows_of(0, d), col) if g == 0 else (rows_of(1, 0), col_at(d))

    def both(g, d, e):
        return (rows_of(0, d), col_at(e)) if g == 0 else (rows_of(1, e), col_at(d))

    def first_to(g, d):
        return {"row": at(d, 0)} if g == 0 else {"col": col_at(d)}

    def second_to(g, d):
        return {"col": col_at(d)} if g == 0 else {"row": at(d, 0)}

    def spread(g, d):
        rows, which = one(g, d)
        send_coef(2, rows, which, y_sem.at[g, 0, d], **second_to(g, 1))
        send_coef(2, rows, which, y_sem.at[g, 1, d], **second_to(g, 3))
        send_coef(4, rows, which, core_sem, col=partner)

    def arrive_first(g, s):
        wait_rows(sizes[g], x_sem.at[g, s - 1])
        spread(g, X - s)

    def arrive_second(g, i, d):
        rows, which = both(g, d, 3)
        wait_rows(sizes[g], y_sem.at[g, 0, d])
        if i < 2:
            send_coef(3, rows, which, relay_sem.at[g, i], **second_to(g, 1))
        send_coef(4, rows, which, core_sem, col=partner)
        rows, which = both(g, d, 1)
        wait_rows(sizes[g], y_sem.at[g, 1, d])
        if i >= 2:
            send_coef(3, rows, which, relay_sem.at[g, i], **second_to(g, 3))
        send_coef(4, rows, which, core_sem, col=partner)

    def arrive_relay(g, i, d):
        rows, which = both(g, d, 2)
        wait_rows(sizes[g], relay_sem.at[g, i])
        send_coef(4, rows, which, core_sem, col=partner)

    order = (0, 3, 1, 2)
    groups = [g for g in range(2) if sizes[g]]
    wait_rows((Z - 1) * nu_loc, z_sem)
    for s in (1, 3, 2):
        for g in groups:
            rows, which = one(g, 0)
            send_coef(1, rows, which, x_sem.at[g, s - 1], **first_to(g, s))
    for g in groups:
        spread(g, 0)
    for s in (1, 3, 2):
        for g in groups[::-1]:
            arrive_first(g, s)
    for i, d in enumerate(order):
        for g in groups:
            arrive_second(g, i, d)
    for i, d in enumerate(order):
        for g in groups:
            arrive_relay(g, i, d)
    half = whole.at[pl.ds(0, Y)]
    pltpu.make_async_copy(half, half, core_sem).wait()

    for m in range(mu_per):
        own = pltpu.make_async_copy(
            masked.at[row * mu_per + m], matrix.at[m, n_rows], own_sem.at[m]
        )
        own.wait()
        most = matrix.at[m, pl.ds(0, (ROWS - 1) * nu_loc)]
        pltpu.make_async_copy(most, most, matrix_sem.at[m]).wait()
        per = aux_loc // nu_loc

        def tile(k, carry):
            t = lax.rem(row // per + k, COLS)
            product = lax.dot_general(
                whole[t], matrix[m], (((0,), (0,)), ((), ())),
                preferred_element_type=jnp.float32,
            )
            result[m, pl.ds(pl.multiple_of(t * aux_loc, aux_loc), aux_loc)] = product.astype(
                jnp.bfloat16
            )
            for j in range(per):
                peer = t * per + j

                @pl.when(peer != row)
                def _():
                    pltpu.make_async_remote_copy(
                        result.at[m, pl.ds(pl.multiple_of(peer * nu_loc, nu_loc), nu_loc)],
                        out.at[row * mu_per + m], send_sem.at[1], out_sem,
                        device_id={"row": peer}, device_id_type=MESH,
                    ).start()

            return carry

        lax.fori_loop(0, COLS, tile, 0)
        pltpu.make_async_copy(
            result.at[m, n_rows], out.at[row * mu_per + m], own_sem.at[m]
        ).start()

    for m in range(mu_per):
        pltpu.make_async_copy(
            result.at[m, n_rows], out.at[row * mu_per + m], own_sem.at[m]
        ).wait()
    most = masked.at[pl.ds(0, (ROWS - 1) * mu_per)]
    pltpu.make_async_copy(most, most, out_sem).wait()
    pltpu.make_async_copy(most, most, send_sem.at[0]).wait()
    pltpu.make_async_copy(most, most, send_sem.at[1]).wait()
    wait_rows((Z - 1) * nu_loc, coef_send.at[0])
    wait_rows((X - 1) * slab, coef_send.at[1])
    quarter = whole.at[pl.ds(0, 2)]
    pltpu.make_async_copy(quarter, quarter, coef_send.at[2]).wait()
    wait_rows(X * slab, coef_send.at[3])
    pltpu.make_async_copy(half, half, coef_send.at[4]).wait()


def per_device(tensor, pattern, coef):
    mu_all, nu_loc, aux_loc = tensor.shape
    inputs = [
        pltpu.with_memory_space_constraint(v, pltpu.HBM) for v in (pattern.T, tensor, coef)
    ]
    mu_per = mu_all // ROWS
    nu_all = nu_loc * ROWS
    dma = pltpu.SemaphoreType.DMA
    return pl.pallas_call(
        kernel,
        out_shape=jax.ShapeDtypeStruct(tensor.shape, jnp.bfloat16),
        in_specs=[
            pl.BlockSpec(memory_space=pltpu.HBM),
            pl.BlockSpec(memory_space=pltpu.HBM),
            pl.BlockSpec(memory_space=pltpu.HBM),
        ],
        out_specs=pl.BlockSpec(memory_space=pl.ANY),
        scratch_shapes=[
            pltpu.SMEM((1, pattern.shape[0]), jnp.int32),
            pltpu.VMEM(tensor.shape, jnp.bfloat16),
            pltpu.VMEM(tensor.shape, jnp.bfloat16),
            pltpu.VMEM((mu_per, nu_all, aux_loc), jnp.bfloat16),
            pltpu.VMEM((COLS, nu_all, aux_loc), jnp.bfloat16),
            pltpu.VMEM((mu_per, nu_all, aux_loc), jnp.bfloat16),
            dma((6,)), dma((mu_per,)), dma((2,)), dma((mu_per,)), dma(()),
            dma((5,)), dma(()), dma((2, 3)), dma((2, 2, 4)), dma((2, 4)), dma(()),
        ],
        compiler_params=pltpu.CompilerParams(
            collective_id=0, has_side_effects=True, vmem_limit_bytes=40 * 1024 * 1024
        ),
    )(*inputs)


def solution(mesh):
    return jax.shard_map(
        per_device,
        mesh=mesh,
        in_specs=(P(None, "row", "col"), P("col", "row"), P("row", "col")),
        out_specs=P(None, "row", "col"),
        check_vma=False,
    )
```

```python
import functools

import jax
import jax.numpy as jnp
from jax import lax
from jax.experimental import pallas as pl
from jax.experimental.pallas import tpu as pltpu
from jax.sharding import PartitionSpec as P

MESH = pl.DeviceIdType.MESH
X, Y, Z, CORES = 4, 4, 8, 2
ROWS, COLS = X * Z, Y * CORES
NEAR = 2
SPLIT = 2 * NEAR + 1
BATCH = 12


def kernel(
    pattern_hbm, tensor, coef, out,
    pattern, raw, masked, matrix, whole, result,
    load_sem, own_sem, send_sem, matrix_sem, out_sem,
    coef_send, z_sem, x_sem, y_sem, relay_sem, core_sem,
):
    atoms = pattern.shape[1]
    blk = tensor.shape[2] // atoms
    mu_all, nu_loc, aux_loc = tensor.shape
    mu_per = mu_all // ROWS
    row, col = lax.axis_index("row"), lax.axis_index("col")
    x, z = row // Z, lax.rem(row, Z)
    y, core = col // CORES, lax.rem(col, CORES)

    def at(dx, dz):
        return lax.rem(x + dx, X) * Z + lax.rem(z + dz, Z)

    def col_at(dy):
        return lax.rem(y + dy, Y) * CORES + core

    partner = y * CORES + (1 - core)

    own_pattern = pltpu.make_async_copy(pattern_hbm, pattern, load_sem.at[5])
    own_pattern.start()
    n_rows = pl.ds(pl.multiple_of(row * nu_loc, nu_loc), nu_loc)
    slab, first = Z * nu_loc, SPLIT * nu_loc

    def z_rows(dz, half=None):
        start = pl.multiple_of(x * slab + lax.rem(dz + NEAR + Z, Z) * nu_loc, nu_loc)
        if half is None:
            return pl.ds(start, nu_loc)
        return pl.ds(pl.multiple_of(start + half * (nu_loc // 2), nu_loc // 2), nu_loc // 2)

    own_coef = pltpu.make_async_copy(coef, whole.at[col, z_rows(0)], load_sem.at[4])
    own_coef.start()
    loads = []
    step = mu_all // 4
    for q in range(4):
        part = pl.ds(q * step, step)
        load = pltpu.make_async_copy(tensor.at[part], raw.at[part], load_sem.at[q])
        load.start()
        loads.append(load)

    barrier = pltpu.get_barrier_semaphore()
    hops = lambda d, n: min(d, n - d)
    peers = [(dx, dz) for dx in range(X) for dz in range(Z) if dx or dz]
    for dx, dz in sorted(peers, key=lambda o: -hops(o[0], X) - hops(o[1], Z)):
        pl.semaphore_signal(barrier, 1, device_id={"row": at(dx, dz)}, device_id_type=MESH)
    for dy in range(1, Y):
        pl.semaphore_signal(barrier, 1, device_id={"col": col_at(dy)}, device_id_type=MESH)
    pl.semaphore_signal(barrier, 1, device_id={"col": partner}, device_id_type=MESH)

    own_pattern.wait()
    lane = lax.broadcasted_iota(jnp.int32, (1, 1, aux_loc), 2)
    keep = jnp.zeros((1, 1, aux_loc), jnp.float32)
    for a in range(atoms):
        here = (lane >= a * blk) & (lane < (a + 1) * blk)
        keep = jnp.where(here, pattern[0, a].astype(jnp.float32), keep)
    keep = keep.astype(jnp.bfloat16)
    own_coef.wait()
    for q in range(4):
        loads[q].wait()

        def mask(i, carry):
            some = pl.ds(q * step + i * 2, 2)
            masked[some] = raw[some] * keep
            return carry

        lax.fori_loop(0, step // 2, mask, 0)
    pl.semaphore_wait(barrier, ROWS - 1 + Y - 1 + 1)

    def send_rows(stage, which, rows, to_rows, sem, **device):
        pltpu.make_async_remote_copy(
            whole.at[which, rows], whole.at[which, to_rows], coef_send.at[stage], sem,
            device_id=device, device_id_type=MESH,
        ).start()

    def send_coef(stage, rows, which, sem, **device):
        send_rows(stage, which, rows, rows, sem, **device)

    def wait_rows(count, sem):
        block = whole.at[0, pl.ds(0, count)]
        pltpu.make_async_copy(block, block, sem).wait()

    for dz in (2, -2, 1, -1):
        send_rows(
            0, col, z_rows(0), z_rows(-dz), z_sem.at[2 + dz], row=at(0, (dz + Z) % Z)
        )

    def send_block(m, k, carry):
        j = lax.rem(k * 27, ROWS)
        dz = lax.rem(j, Z)
        peer = at(j // Z, dz)
        pltpu.make_async_remote_copy(
            masked.at[peer * mu_per + m], matrix.at[m, z_rows(-dz)], send_sem.at[0],
            matrix_sem.at[m], device_id={"row": peer}, device_id_type=MESH,
        ).start()
        return carry

    lax.fori_loop(1, 1 + BATCH, functools.partial(send_block, 0), 0)

    for s, half in ((2, 0), (-2, 1)):
        wait_rows(nu_loc, z_sem.at[2 + s])
        d = s // 2
        send_rows(0, col, z_rows(-s), z_rows(-s - d), z_sem.at[5], row=at(0, d % Z))
        send_rows(
            0, col, z_rows(-s, half), z_rows(-2 * s, half), z_sem.at[5], row=at(0, s % Z)
        )
    for m in range(mu_per):
        lax.fori_loop(1 + (BATCH if m == 0 else 0), ROWS, functools.partial(send_block, m), 0)
        pltpu.make_async_copy(
            masked.at[row * mu_per + m], matrix.at[m, z_rows(0)], own_sem.at[m]
        ).start()

    sizes = (first, slab - first)

    def rows_of(g, dx):
        start = lax.rem(x + dx, X) * slab + g * first
        return pl.ds(pl.multiple_of(start, nu_loc), sizes[g])

    def one(g, d):
        return (rows_of(0, d), col) if g == 0 else (rows_of(1, 0), col_at(d))

    def both(g, d, e):
        return (rows_of(0, d), col_at(e)) if g == 0 else (rows_of(1, e), col_at(d))

    def first_to(g, d):
        return {"row": at(d, 0)} if g == 0 else {"col": col_at(d)}

    def second_to(g, d):
        return {"col": col_at(d)} if g == 0 else {"row": at(d, 0)}

    def spread(g, d):
        rows, which = one(g, d)
        send_coef(2, rows, which, y_sem.at[g, 0, d], **second_to(g, 1))
        send_coef(2, rows, which, y_sem.at[g, 1, d], **second_to(g, 3))
        send_coef(4, rows, which, core_sem, col=partner)

    def arrive_first(g, s):
        wait_rows(sizes[g], x_sem.at[g, s - 1])
        spread(g, X - s)

    def arrive_second(g, i, d):
        rows, which = both(g, d, 3)
        wait_rows(sizes[g], y_sem.at[g, 0, d])
        if i < 2:
            send_coef(3, rows, which, relay_sem.at[g, i], **second_to(g, 1))
        send_coef(4, rows, which, core_sem, col=partner)
        rows, which = both(g, d, 1)
        wait_rows(sizes[g], y_sem.at[g, 1, d])
        if i >= 2:
            send_coef(3, rows, which, relay_sem.at[g, i], **second_to(g, 3))
        send_coef(4, rows, which, core_sem, col=partner)

    def arrive_relay(g, i, d):
        rows, which = both(g, d, 2)
        wait_rows(sizes[g], relay_sem.at[g, i])
        send_coef(4, rows, which, core_sem, col=partner)

    def begin(g):
        rows, which = one(g, 0)
        for s in (1, 3, 2):
            send_coef(1, rows, which, x_sem.at[g, s - 1], **first_to(g, s))
        spread(g, 0)

    order = (0, 3, 1, 2)
    groups = (0, 1)
    for s in (1, -1):
        wait_rows(nu_loc, z_sem.at[2 + s])
    begin(0)
    wait_rows((Z - SPLIT) * nu_loc, z_sem.at[5])
    begin(1)
    for s in (1, 3, 2):
        for g in groups[::-1]:
            arrive_first(g, s)
    for i, d in enumerate(order):
        for g in groups:
            arrive_second(g, i, d)
    for i, d in enumerate(order):
        for g in groups:
            arrive_relay(g, i, d)
    half = whole.at[pl.ds(0, Y)]
    pltpu.make_async_copy(half, half, core_sem).wait()

    for m in range(mu_per):
        own = pltpu.make_async_copy(
            masked.at[row * mu_per + m], matrix.at[m, z_rows(0)], own_sem.at[m]
        )
        own.wait()
        most = matrix.at[m, pl.ds(0, (ROWS - 1) * nu_loc)]
        pltpu.make_async_copy(most, most, matrix_sem.at[m]).wait()
        per = aux_loc // nu_loc

        def tile(k, carry):
            t = lax.rem(row // per + k, COLS)
            product = lax.dot_general(
                whole[t], matrix[m], (((0,), (0,)), ((), ())),
                preferred_element_type=jnp.float32,
            )
            result[m, pl.ds(pl.multiple_of(t * aux_loc, aux_loc), aux_loc)] = product.astype(
                jnp.bfloat16
            )
            for j in range(per):
                peer = t * per + j

                @pl.when(peer != row)
                def _():
                    pltpu.make_async_remote_copy(
                        result.at[m, pl.ds(pl.multiple_of(peer * nu_loc, nu_loc), nu_loc)],
                        out.at[row * mu_per + m], send_sem.at[1], out_sem,
                        device_id={"row": peer}, device_id_type=MESH,
                    ).start()

            return carry

        lax.fori_loop(0, COLS, tile, 0)
        pltpu.make_async_copy(
            result.at[m, n_rows], out.at[row * mu_per + m], own_sem.at[m]
        ).start()

    for m in range(mu_per):
        pltpu.make_async_copy(
            result.at[m, n_rows], out.at[row * mu_per + m], own_sem.at[m]
        ).wait()
    most = masked.at[pl.ds(0, (ROWS - 1) * mu_per)]
    pltpu.make_async_copy(most, most, out_sem).wait()
    pltpu.make_async_copy(most, most, send_sem.at[0]).wait()
    pltpu.make_async_copy(most, most, send_sem.at[1]).wait()
    wait_rows((Z - 1) * nu_loc, coef_send.at[0])
    wait_rows((X - 1) * slab, coef_send.at[1])
    quarter = whole.at[pl.ds(0, 2)]
    pltpu.make_async_copy(quarter, quarter, coef_send.at[2]).wait()
    wait_rows(X * slab, coef_send.at[3])
    pltpu.make_async_copy(half, half, coef_send.at[4]).wait()


def per_device(tensor, pattern, coef):
    mu_all, nu_loc, aux_loc = tensor.shape
    inputs = [
        pltpu.with_memory_space_constraint(v, pltpu.HBM) for v in (pattern.T, tensor, coef)
    ]
    mu_per = mu_all // ROWS
    nu_all = nu_loc * ROWS
    dma = pltpu.SemaphoreType.DMA
    return pl.pallas_call(
        kernel,
        out_shape=jax.ShapeDtypeStruct(tensor.shape, jnp.bfloat16),
        in_specs=[
            pl.BlockSpec(memory_space=pltpu.HBM),
            pl.BlockSpec(memory_space=pltpu.HBM),
            pl.BlockSpec(memory_space=pltpu.HBM),
        ],
        out_specs=pl.BlockSpec(memory_space=pl.ANY),
        scratch_shapes=[
            pltpu.SMEM((1, pattern.shape[0]), jnp.int32),
            pltpu.VMEM(tensor.shape, jnp.bfloat16),
            pltpu.VMEM(tensor.shape, jnp.bfloat16),
            pltpu.VMEM((mu_per, nu_all, aux_loc), jnp.bfloat16),
            pltpu.VMEM((COLS, nu_all, aux_loc), jnp.bfloat16),
            pltpu.VMEM((mu_per, nu_all, aux_loc), jnp.bfloat16),
            dma((6,)), dma((mu_per,)), dma((2,)), dma((mu_per,)), dma(()),
            dma((5,)), dma((6,)), dma((2, 3)), dma((2, 2, 4)), dma((2, 4)), dma(()),
        ],
        compiler_params=pltpu.CompilerParams(
            collective_id=0, has_side_effects=True, vmem_limit_bytes=40 * 1024 * 1024
        ),
    )(*inputs)


def solution(mesh):
    return jax.shard_map(
        per_device,
        mesh=mesh,
        in_specs=(P(None, "row", "col"), P("col", "row"), P("row", "col")),
        out_specs=P(None, "row", "col"),
        check_vma=False,
    )
```

```python
import functools

import jax
import jax.numpy as jnp
from jax import lax
from jax.experimental import pallas as pl
from jax.experimental.pallas import tpu as pltpu
from jax.sharding import PartitionSpec as P

MESH = pl.DeviceIdType.MESH
X, Y, Z, CORES = 4, 4, 8, 2
ROWS, COLS = X * Z, Y * CORES
NEAR = 2
SPLIT = 2 * NEAR + 1
BATCH = 14


def kernel(
    pattern_hbm, tensor, coef, out,
    pattern, raw, masked, matrix, whole, result,
    load_sem, own_sem, send_sem, matrix_sem, out_sem,
    coef_send, z_sem, x_sem, y_sem, relay_sem, core_sem,
):
    atoms = pattern.shape[1]
    blk = tensor.shape[2] // atoms
    mu_all, nu_loc, aux_loc = tensor.shape
    mu_per = mu_all // ROWS
    row, col = lax.axis_index("row"), lax.axis_index("col")
    x, z = row // Z, lax.rem(row, Z)
    y, core = col // CORES, lax.rem(col, CORES)

    def at(dx, dz):
        return lax.rem(x + dx, X) * Z + lax.rem(z + dz, Z)

    def col_at(dy):
        return lax.rem(y + dy, Y) * CORES + core

    partner = y * CORES + (1 - core)

    own_pattern = pltpu.make_async_copy(pattern_hbm, pattern, load_sem.at[5])
    own_pattern.start()
    n_rows = pl.ds(pl.multiple_of(row * nu_loc, nu_loc), nu_loc)
    slab, first = Z * nu_loc, SPLIT * nu_loc

    def z_rows(dz, half=None):
        start = pl.multiple_of(x * slab + lax.rem(dz + NEAR + Z, Z) * nu_loc, nu_loc)
        if half is None:
            return pl.ds(start, nu_loc)
        return pl.ds(pl.multiple_of(start + half * (nu_loc // 2), nu_loc // 2), nu_loc // 2)

    own_coef = pltpu.make_async_copy(coef, whole.at[col, z_rows(0)], load_sem.at[4])
    own_coef.start()
    loads = []
    step = mu_all // 4
    for q in range(4):
        part = pl.ds(q * step, step)
        load = pltpu.make_async_copy(tensor.at[part], raw.at[part], load_sem.at[q])
        load.start()
        loads.append(load)

    barrier = pltpu.get_barrier_semaphore()
    hops = lambda d, n: min(d, n - d)
    peers = [(dx, dz) for dx in range(X) for dz in range(Z) if dx or dz]
    for dx, dz in sorted(peers, key=lambda o: -hops(o[0], X) - hops(o[1], Z)):
        pl.semaphore_signal(barrier, 1, device_id={"row": at(dx, dz)}, device_id_type=MESH)
    for dy in range(1, Y):
        pl.semaphore_signal(barrier, 1, device_id={"col": col_at(dy)}, device_id_type=MESH)
    pl.semaphore_signal(barrier, 1, device_id={"col": partner}, device_id_type=MESH)

    own_pattern.wait()
    lane = lax.broadcasted_iota(jnp.int32, (1, 1, aux_loc), 2)
    keep = jnp.zeros((1, 1, aux_loc), jnp.float32)
    for a in range(atoms):
        here = (lane >= a * blk) & (lane < (a + 1) * blk)
        keep = jnp.where(here, pattern[0, a].astype(jnp.float32), keep)
    keep = keep.astype(jnp.bfloat16)
    own_coef.wait()
    for q in range(4):
        loads[q].wait()

        def mask(i, carry):
            some = pl.ds(q * step + i * 2, 2)
            masked[some] = raw[some] * keep
            return carry

        lax.fori_loop(0, step // 2, mask, 0)
    pl.semaphore_wait(barrier, ROWS - 1 + Y - 1 + 1)

    def send_rows(stage, which, rows, to_rows, sem, **device):
        pltpu.make_async_remote_copy(
            whole.at[which, rows], whole.at[which, to_rows], coef_send.at[stage], sem,
            device_id=device, device_id_type=MESH,
        ).start()

    def send_coef(stage, rows, which, sem, **device):
        send_rows(stage, which, rows, rows, sem, **device)

    def wait_rows(count, sem):
        block = whole.at[0, pl.ds(0, count)]
        pltpu.make_async_copy(block, block, sem).wait()

    for dz in (2, -2, 1, -1):
        send_rows(
            0, col, z_rows(0), z_rows(-dz), z_sem.at[2 + dz], row=at(0, (dz + Z) % Z)
        )

    def send_block(m, k, carry):
        j = lax.rem(k * 27, ROWS)
        dz = lax.rem(j, Z)
        peer = at(j // Z, dz)
        pltpu.make_async_remote_copy(
            masked.at[peer * mu_per + m], matrix.at[m, z_rows(-dz)], send_sem.at[0],
            matrix_sem.at[m], device_id={"row": peer}, device_id_type=MESH,
        ).start()
        return carry

    lax.fori_loop(1, 1 + 10, functools.partial(send_block, 0), 0)

    for s, half in ((2, 0), (-2, 1)):
        if s < 0:
            lax.fori_loop(1 + 10, 1 + BATCH, functools.partial(send_block, 0), 0)
        wait_rows(nu_loc, z_sem.at[2 + s])
        d = s // 2
        send_rows(0, col, z_rows(-s), z_rows(-s - d), z_sem.at[5], row=at(0, d % Z))
        send_rows(
            0, col, z_rows(-s, half), z_rows(-2 * s, half), z_sem.at[5], row=at(0, s % Z)
        )
    for m in range(mu_per):
        lax.fori_loop(1 + (BATCH if m == 0 else 0), ROWS, functools.partial(send_block, m), 0)
        pltpu.make_async_copy(
            masked.at[row * mu_per + m], matrix.at[m, z_rows(0)], own_sem.at[m]
        ).start()

    sizes = (first, slab - first)

    def rows_of(g, dx):
        start = lax.rem(x + dx, X) * slab + g * first
        return pl.ds(pl.multiple_of(start, nu_loc), sizes[g])

    def one(g, d):
        return (rows_of(0, d), col) if g == 0 else (rows_of(1, 0), col_at(d))

    def both(g, d, e):
        return (rows_of(0, d), col_at(e)) if g == 0 else (rows_of(1, e), col_at(d))

    def first_to(g, d):
        return {"row": at(d, 0)} if g == 0 else {"col": col_at(d)}

    def second_to(g, d):
        return {"col": col_at(d)} if g == 0 else {"row": at(d, 0)}

    def spread(g, d):
        rows, which = one(g, d)
        send_coef(2, rows, which, y_sem.at[g, 0, d], **second_to(g, 1))
        send_coef(2, rows, which, y_sem.at[g, 1, d], **second_to(g, 3))
        send_coef(4, rows, which, core_sem, col=partner)

    def arrive_first(g, s):
        wait_rows(sizes[g], x_sem.at[g, s - 1])
        spread(g, X - s)

    def arrive_second(g, i, d):
        rows, which = both(g, d, 3)
        wait_rows(sizes[g], y_sem.at[g, 0, d])
        if i < 2:
            send_coef(3, rows, which, relay_sem.at[g, i], **second_to(g, 1))
        send_coef(4, rows, which, core_sem, col=partner)
        rows, which = both(g, d, 1)
        wait_rows(sizes[g], y_sem.at[g, 1, d])
        if i >= 2:
            send_coef(3, rows, which, relay_sem.at[g, i], **second_to(g, 3))
        send_coef(4, rows, which, core_sem, col=partner)

    def arrive_relay(g, i, d):
        rows, which = both(g, d, 2)
        wait_rows(sizes[g], relay_sem.at[g, i])
        send_coef(4, rows, which, core_sem, col=partner)

    def begin(g):
        rows, which = one(g, 0)
        for s in (1, 3, 2):
            send_coef(1, rows, which, x_sem.at[g, s - 1], **first_to(g, s))
        spread(g, 0)

    order = (0, 3, 1, 2)
    groups = (0, 1)
    for s in (1, -1):
        wait_rows(nu_loc, z_sem.at[2 + s])
    begin(0)
    wait_rows((Z - SPLIT) * nu_loc, z_sem.at[5])
    begin(1)
    for s in (1, 3, 2):
        for g in groups[::-1]:
            arrive_first(g, s)
    for i, d in enumerate(order):
        for g in groups:
            arrive_second(g, i, d)
    for i, d in enumerate(order):
        for g in groups:
            arrive_relay(g, i, d)
    half = whole.at[pl.ds(0, Y)]
    pltpu.make_async_copy(half, half, core_sem).wait()

    for m in range(mu_per):
        own = pltpu.make_async_copy(
            masked.at[row * mu_per + m], matrix.at[m, z_rows(0)], own_sem.at[m]
        )
        own.wait()
        most = matrix.at[m, pl.ds(0, (ROWS - 1) * nu_loc)]
        pltpu.make_async_copy(most, most, matrix_sem.at[m]).wait()
        per = aux_loc // nu_loc

        def tile(k, carry):
            t = lax.rem(row // per + k, COLS)
            product = lax.dot_general(
                whole[t], matrix[m], (((0,), (0,)), ((), ())),
                preferred_element_type=jnp.float32,
            )
            result[m, pl.ds(pl.multiple_of(t * aux_loc, aux_loc), aux_loc)] = product.astype(
                jnp.bfloat16
            )
            for j in range(per):
                peer = t * per + j

                @pl.when(peer != row)
                def _():
                    pltpu.make_async_remote_copy(
                        result.at[m, pl.ds(pl.multiple_of(peer * nu_loc, nu_loc), nu_loc)],
                        out.at[row * mu_per + m], send_sem.at[1], out_sem,
                        device_id={"row": peer}, device_id_type=MESH,
                    ).start()

            return carry

        lax.fori_loop(0, COLS, tile, 0)
        pltpu.make_async_copy(
            result.at[m, n_rows], out.at[row * mu_per + m], own_sem.at[m]
        ).start()

    for m in range(mu_per):
        pltpu.make_async_copy(
            result.at[m, n_rows], out.at[row * mu_per + m], own_sem.at[m]
        ).wait()
    most = masked.at[pl.ds(0, (ROWS - 1) * mu_per)]
    pltpu.make_async_copy(most, most, out_sem).wait()
    pltpu.make_async_copy(most, most, send_sem.at[0]).wait()
    pltpu.make_async_copy(most, most, send_sem.at[1]).wait()
    wait_rows((Z - 1) * nu_loc, coef_send.at[0])
    wait_rows((X - 1) * slab, coef_send.at[1])
    quarter = whole.at[pl.ds(0, 2)]
    pltpu.make_async_copy(quarter, quarter, coef_send.at[2]).wait()
    wait_rows(X * slab, coef_send.at[3])
    pltpu.make_async_copy(half, half, coef_send.at[4]).wait()


def per_device(tensor, pattern, coef):
    mu_all, nu_loc, aux_loc = tensor.shape
    inputs = [
        pltpu.with_memory_space_constraint(v, pltpu.HBM) for v in (pattern.T, tensor, coef)
    ]
    mu_per = mu_all // ROWS
    nu_all = nu_loc * ROWS
    dma = pltpu.SemaphoreType.DMA
    return pl.pallas_call(
        kernel,
        out_shape=jax.ShapeDtypeStruct(tensor.shape, jnp.bfloat16),
        in_specs=[
            pl.BlockSpec(memory_space=pltpu.HBM),
            pl.BlockSpec(memory_space=pltpu.HBM),
            pl.BlockSpec(memory_space=pltpu.HBM),
        ],
        out_specs=pl.BlockSpec(memory_space=pl.ANY),
        scratch_shapes=[
            pltpu.SMEM((1, pattern.shape[0]), jnp.int32),
            pltpu.VMEM(tensor.shape, jnp.bfloat16),
            pltpu.VMEM(tensor.shape, jnp.bfloat16),
            pltpu.VMEM((mu_per, nu_all, aux_loc), jnp.bfloat16),
            pltpu.VMEM((COLS, nu_all, aux_loc), jnp.bfloat16),
            pltpu.VMEM((mu_per, nu_all, aux_loc), jnp.bfloat16),
            dma((6,)), dma((mu_per,)), dma((2,)), dma((mu_per,)), dma(()),
            dma((5,)), dma((6,)), dma((2, 3)), dma((2, 2, 4)), dma((2, 4)), dma(()),
        ],
        compiler_params=pltpu.CompilerParams(
            collective_id=0, has_side_effects=True, vmem_limit_bytes=40 * 1024 * 1024
        ),
    )(*inputs)


def solution(mesh):
    return jax.shard_map(
        per_device,
        mesh=mesh,
        in_specs=(P(None, "row", "col"), P("col", "row"), P("row", "col")),
        out_specs=P(None, "row", "col"),
        check_vma=False,
    )
```
